32 devices in a mesh: shell: 4 (over y, core), img: 8 (over z, x).
Axes of the slice: x: 2, y: 2, z: 4, core: 2. Of those that a mesh axis runs over, the one named last changes fastest.
Arguments:
- images: bfloat16 [6144, 16384], P('img', 'shell'), may hold values from -12 to 12, as said below
- references: bfloat16 [256, 16384], P('img', 'shell'), may hold values from -1 to 1, as said below
- shell_of_pixel: int32 [16384], P('shell'), may hold values from 0 to 63
- noise_power: float32 [64], replicated, may hold values from 0.1 to 10
- ref_class: int32 [256], replicated, may hold values from 0 to 3
- ref_orient: int32 [256], replicated, may hold values from 0 to 6143
- class_logw: float32 [4], replicated, may hold values from -4 to 4
- orient_logw: float32 [6144], replicated, may hold values from -4 to 4
Outputs:
- accumulators: float32 [256, 16384], P('img', 'shell')
- evidence_logarithm: float32 [6144], P('img')
The draws below stay inside these ranges and needn't reach their ends.
Inputs may be any that keep to these rules, and one draw needn't show every extreme that they name: `images`: images are real-valued Fourier data. `references`: references are real-valued projections.
All inputs are finite; a program needn't handle non-finite values.
Results may differ from the reference program's by a relative error of at most 0.0077.
Values may be sent and summed in bfloat16 or wider, within the bound.
No kernel may reach another device: no remote copies, remote signals or barrier semaphores. Data moves between devices by JAX's collectives and lax.ppermute only.
A program may use at most 128 MiB of HBM per device.

```python
import math
import jax
import jax.numpy as jnp
from jax import lax

PIX = 16384
NSHELL = 64
NCLASS = 4
NORIENT = 6144
NREF = 256
NIMG = 6144


def joint_draw(key):
    folded = jax.random.fold_in(key, 7001)
    subkeys = jax.random.split(folded, 3)
    row_scale = jnp.exp(jax.random.uniform(subkeys[0], (NREF, 1), jnp.float32, jnp.log(0.5), jnp.log(2.5)))
    reference_pixels = jax.random.normal(subkeys[1], (NREF, PIX), jnp.float32) * row_scale / jnp.sqrt(jnp.float32(PIX))
    image_data = jax.random.normal(subkeys[2], (NIMG, PIX), jnp.float32)
    return (jnp.clip(image_data, -12.0, 12.0), jnp.clip(reference_pixels, -1.0, 1.0))


def draw_images(key, part):
    return joint_draw(key)[0].astype(jnp.bfloat16)


def draw_references(key, part):
    return joint_draw(key)[1].astype(jnp.bfloat16)


def with_ends(entries, own_key, low, top_value):
    place = [jax.random.randint(jax.random.fold_in(own_key, axis), (), 0, length) for axis, length in enumerate(entries.shape)]
    widest = entries.shape.index(max(entries.shape))
    beside = place[:widest] + [(place[widest] + 1) % entries.shape[widest]] + place[widest + 1:]
    return entries.at[tuple(place)].set(low).at[tuple(beside)].set(top_value)


def gaussian(key, dims, width, bound, held_as=jnp.bfloat16):
    array = jax.random.normal(key, dims, jnp.float32) * width
    return jnp.minimum(jnp.maximum(array, -bound), bound).astype(held_as)


def setup_inputs(seed: int = 0) -> dict:
    key_list = jax.random.split(jax.random.key(seed), 9)
    return {
        "images": draw_images(jax.random.fold_in(key_list[8], 71), 0),
        "references": draw_references(jax.random.fold_in(key_list[8], 71), 0),
        "shell_of_pixel": with_ends(jax.random.randint(key_list[2], (PIX,), 0, NSHELL), jax.random.fold_in(key_list[2], 1), 0, NSHELL - 1).astype(jnp.int32),
        "noise_power": jnp.clip(jnp.exp(jax.random.uniform(key_list[3], (NSHELL,), jnp.float32, math.log(0.1), math.log(10.0))), 0.1, 10.0),
        "ref_class": with_ends(jax.random.randint(key_list[4], (NREF,), 0, NCLASS), jax.random.fold_in(key_list[4], 1), 0, NCLASS - 1).astype(jnp.int32),
        "ref_orient": with_ends(jax.random.randint(key_list[5], (NREF,), 0, NORIENT), jax.random.fold_in(key_list[5], 1), 0, NORIENT - 1).astype(jnp.int32),
        "class_logw": gaussian(key_list[6], (NCLASS,), 1.0, 4.0, jnp.float32),
        "orient_logw": gaussian(key_list[7], (NORIENT,), 1.0, 4.0, jnp.float32),
    }


inverse_heat_factor = 0.5


def reference(images, references, shell_of_pixel, noise_power, ref_class, ref_orient, class_logw, orient_logw):
    inverse_noise = 1.0 / noise_power
    matches = shell_of_pixel[:, None] == jnp.arange(NSHELL, dtype=jnp.int32)[None, :]
    weights = jnp.sum(jnp.where(matches, inverse_noise[None, :], jnp.float32(0.0)), axis=1)
    weighted = (images.astype(jnp.float32) * weights[None, :]).astype(jnp.bfloat16)
    ref_float = references.astype(jnp.float32)
    ref_norm = jnp.dot(ref_float * ref_float, weights, precision=lax.Precision.HIGHEST)
    correlation = jnp.dot(weighted, references.T, preferred_element_type=jnp.float32)
    agreement_measures = correlation - 0.5 * ref_norm[None, :]
    class_agreement = ref_class[:, None] == jnp.arange(NCLASS, dtype=jnp.int32)[None, :]
    beforehand_logarithmic_share = jnp.sum(jnp.where(class_agreement, class_logw[None, :], jnp.float32(0.0)), axis=1) + orient_logw[ref_orient]
    raw_logarithmic_measures = inverse_heat_factor * agreement_measures + beforehand_logarithmic_share[None, :]
    highest = jnp.max(raw_logarithmic_measures, axis=1)
    evidence_logarithm = highest + jnp.log(jnp.sum(jnp.exp(raw_logarithmic_measures - highest[:, None]), axis=1))
    posterior = jnp.exp(raw_logarithmic_measures - evidence_logarithm[:, None]).astype(jnp.bfloat16)
    accumulators = jnp.dot(posterior.T, images, preferred_element_type=jnp.float32)
    return accumulators, evidence_logarithm
```

```python
import jax
import jax.numpy as jnp
from jax import lax
from jax.sharding import PartitionSpec as P

inverse_heat_factor = 0.5


def partners(size, step):
    if size & (size - 1) == 0:
        return [i ^ step for i in range(size)]
    return [(i + step) % size for i in range(size)]


def make_shards(n_img, n_shell):
    inner = 2 if n_img % 2 == 0 else 1
    outer = n_img // inner
    cores = 2 if n_shell % 2 == 0 else 1
    chips = n_shell // cores

    def outer_pairs(step, back=False):
        to = partners(outer, step)
        pairs = [(o * inner + i, to[o] * inner + i) for o in range(outer) for i in range(inner)]
        return [(b, a) for a, b in pairs] if back else pairs

    inner_pairs = [(k, k ^ 1) for k in range(n_img)]
    core_pairs = [(k, k ^ 1) for k in range(n_shell)]

    def chip_pairs(step):
        to = partners(chips, step)
        return [(o * cores + i, to[o] * cores + i) for o in range(chips) for i in range(cores)]

    def swap_inner(a):
        return lax.ppermute(a, "img", inner_pairs)

    def shards(
        images, references, shell_of_pixel, noise_power, ref_class, ref_orient, class_logw, orient_logw
    ):
        rows, pixels = images.shape
        block = references.shape[0]
        half = rows // cores
        core = lax.axis_index("shell") % cores
        me = lax.axis_index("img")
        my_outer, my_inner = me // inner, me % inner

        steps = [s for s in range(outer - 1, 0, -1)]
        got = {0: references}
        if inner == 2:
            crossed = {0: swap_inner(references)}
        for s in sorted(steps, key=lambda s: (s & 1, -s)):
            got[s] = lax.ppermute(references, "img", outer_pairs(s))
        if inner == 2:
            for s in range(1, outer):
                crossed[s] = swap_inner(got[s])

        inverse_noise = 1.0 / noise_power
        matches = shell_of_pixel[:, None] == jnp.arange(noise_power.shape[0], dtype=jnp.int32)[None, :]
        weights = jnp.sum(jnp.where(matches, inverse_noise[None, :], jnp.float32(0.0)), axis=1)
        weighted = (images.astype(jnp.float32) * weights[None, :]).astype(jnp.bfloat16)
        if cores == 2:
            kept = lax.dynamic_slice_in_dim(weighted, core * half, half, 0)
            given = lax.dynamic_slice_in_dim(weighted, (1 - core) * half, half, 0)

        class_agreement = (
            ref_class[:, None] == jnp.arange(class_logw.shape[0], dtype=jnp.int32)[None, :]
        )
        log_prior = (
            jnp.sum(jnp.where(class_agreement, class_logw[None, :], jnp.float32(0.0)), axis=1)
            + orient_logw[ref_orient]
        ).reshape(n_img, block)

        def owner(s, i):
            if outer & (outer - 1) == 0:
                o = my_outer ^ s
            else:
                o = (my_outer - s) % outer
            return o * inner + (my_inner ^ i if inner == 2 else 0)

        groups = [[0, 1] if outer > 1 else [0]]
        groups += [[s] for s in range(2, outer)]
        if outer > 4:
            groups = [list(range(outer // 2)), list(range(outer // 2, outer - 1)), [outer - 1]]
        order = []
        totals = []
        for g in groups:
            slots = [(s, i) for s in g for i in range(inner)]
            order += slots
            refs = jnp.concatenate([got[s] if i == 0 else crossed[s] for s, i in slots], axis=0)
            as_float = refs.astype(jnp.float32)
            norm = 0.5 * jnp.sum(as_float * as_float * weights[None, :], axis=1)

            def partial(side):
                return (
                    lax.dot_general(
                        side, refs, (((1,), (1,)), ((), ())), preferred_element_type=jnp.float32
                    )
                    - norm[None, :]
                )

            if cores == 2:
                from_core = lax.ppermute(partial(given), "shell", core_pairs)
                mine = partial(kept) + from_core
            else:
                mine = partial(weighted)
            total = mine
            for s in range(1, chips):
                total = total + lax.ppermute(mine, "shell", chip_pairs(s))
            totals.append(total)
        scores = jnp.concatenate(totals, axis=1)
        prior = jnp.concatenate(
            [lax.dynamic_index_in_dim(log_prior, owner(s, i), 0, False) for s, i in order]
        )

        logits = inverse_heat_factor * scores + prior[None, :]
        highest = jnp.max(logits, axis=1)
        evidence = highest + jnp.log(jnp.sum(jnp.exp(logits - highest[:, None]), axis=1))
        posterior = jnp.exp(logits - evidence[:, None]).astype(jnp.bfloat16)
        if cores == 2:
            other_posterior = lax.ppermute(posterior, "shell", core_pairs)
            other_evidence = lax.ppermute(evidence, "shell", core_pairs)
            first = core == 0
            posterior = jnp.concatenate(
                [
                    jnp.where(first, posterior, other_posterior),
                    jnp.where(first, other_posterior, posterior),
                ]
            )
            evidence = jnp.concatenate(
                [jnp.where(first, evidence, other_evidence), jnp.where(first, other_evidence, evidence)]
            )

        chunks = 2
        width = pixels // chunks
        place = {slot: k for k, slot in enumerate(order)}
        outs = []
        for c in range(chunks):
            part = lax.slice_in_dim(images, c * width, (c + 1) * width, axis=1)
            sums = lax.dot_general(
                posterior, part, (((0,), (0,)), ((), ())), preferred_element_type=jnp.float32
            ).reshape(n_img, block, width)

            def combined(s):
                own = sums[place[(s, 0)]]
                if inner == 2:
                    own = own + swap_inner(sums[place[(s, 1)]].astype(jnp.bfloat16)).astype(jnp.float32)
                return own

            arrived = [
                lax.ppermute(combined(s).astype(jnp.bfloat16), "img", outer_pairs(s, back=True))
                for s in range(outer - 1, 0, -1)
            ]
            out = combined(0)
            for a in arrived:
                out = out + a.astype(jnp.float32)
            outs.append(out)
        return (jnp.concatenate(outs, axis=1), evidence)

    return shards


def solution(mesh):
    placed = (P("img", "shell"), P("img", "shell"), P("shell"), P(), P(), P(), P(), P())
    return jax.shard_map(
        make_shards(mesh.shape["img"], mesh.shape["shell"]),
        mesh=mesh,
        in_specs=placed,
        out_specs=(P("img", "shell"), P("img")),
        check_vma=False,
    )
```
